32 devices in a mesh: beam: 1, freq: 32 (over z, y, x, core), tm: 1.
Axes of the slice: x: 2, y: 2, z: 4, core: 2. Of those that a mesh axis runs over, the one named last changes fastest.
Arguments:
- data: bfloat16 [4096, 640], P(('beam', 'freq'), 'tm'), may hold values from -1000 to 1000
- chan_delay: int32 [64, 4096], P(None, 'freq'), may hold values from 0 to 40, as said below
- sub_delay: int32 [2048, 64], P('freq'), may hold values from 0 to 24, as said below
- widths: int32 [16], replicated, may hold values from 1 to 256, as said below
Outputs:
- snr: float32 [2048, 16], P(('beam', 'freq'))
The draws below stay inside these ranges and needn't reach their ends.
Inputs may be any that keep to these rules, and one draw needn't show every extreme that they name: chan_delay[s, c] is never smaller for a larger trial s; the value 40 is reached. sub_delay[d, b] is never smaller for a larger trial d; the value 24 is reached. The widths are distinct and include 1 and 256.
All inputs are finite; a program needn't handle non-finite values.
Results may differ from the reference program's by a relative error of at most 0.0014.
Values may be sent and summed in bfloat16 or wider, within the bound.
A program may use at most 64 MiB of HBM per device.

```python
import math
import jax
import jax.numpy as jnp
from jax import lax

NCHAN = 4096
NSUB = 64
NSDM = 64
NDM = 2048
WMAX = 256
NW = 16
CPS = 64
DPS = 32
D1MAX = 40
D2MAX = 24
NT = 640


def draw_data(key, part):
    k_noise, k_gain, k_base = jax.random.split(key, 3)
    gain = jnp.exp(jax.random.uniform(k_gain, (NCHAN, 1), jnp.float32, 0.0, math.log(10.0)))
    times = jnp.arange(NT, dtype=jnp.float32)[None, :] / NT
    noise = jnp.clip(jax.random.normal(k_noise, (NCHAN, NT), jnp.float32), -5.0, 5.0)
    envelope = 3.0 ** times
    baseline = 0.5 * jnp.clip(jax.random.normal(k_base, (NCHAN, 1), jnp.float32), -3.0, 3.0)
    return (gain * (envelope * noise + baseline)).astype(jnp.bfloat16)


def draw_chan_delay(key, part):
    k_steps, k_top = jax.random.split(key, 2)
    increments = jax.random.randint(k_steps, (NSUB, CPS), 1, 5)
    column = jnp.arange(CPS, dtype=jnp.int32)[None, :]
    increments = jnp.where(column == 0, 0, increments)
    curve = jnp.cumsum(increments, axis=1)
    tops = jax.random.randint(k_top, (NSUB,), D1MAX // 2, D1MAX + 1)
    band = jnp.arange(NSUB, dtype=jnp.int32)
    tops = jnp.where(band == 0, D1MAX, tops).astype(jnp.int32)
    trial = jnp.arange(1, NSDM + 1, dtype=jnp.int32)
    delay = trial[:, None, None] * curve[None, :, :] * tops[None, :, None] // (NSDM * curve[None, :, CPS - 1:CPS])
    return delay.reshape(NSDM, NCHAN).astype(jnp.int32)


def draw_sub_delay(key, part):
    increments = jax.random.randint(key, (NSUB,), 1, 5)
    column = jnp.arange(NSUB, dtype=jnp.int32)
    increments = jnp.where(column == 0, 0, increments)
    curve = jnp.cumsum(increments)
    trial = jnp.arange(1, NDM + 1, dtype=jnp.int32)
    delay = trial[:, None] * curve[None, :] * D2MAX // (NDM * curve[NSUB - 1])
    return delay.astype(jnp.int32)


def draw_widths(key, part):
    chosen = jax.random.permutation(key, WMAX - 2)[:NW - 2] + 2
    first = jnp.ones((1,), jnp.int32)
    last = jnp.full((1,), WMAX, jnp.int32)
    return jnp.concatenate([first, chosen.astype(jnp.int32), last]).astype(jnp.int32)


def setup_inputs(seed: int = 0, part: int = 0) -> dict:
    arg_keys = jax.random.split(jax.random.key(seed), 5)
    part_keys = jax.random.split(jax.random.fold_in(arg_keys[4], part), 5)
    return {
        "data": draw_data(jax.random.fold_in(jax.random.fold_in(arg_keys[4], part), 71), part),
        "chan_delay": draw_chan_delay(jax.random.fold_in(arg_keys[4], 71), part),
        "sub_delay": draw_sub_delay(jax.random.fold_in(arg_keys[4], 71), part),
        "widths": draw_widths(jax.random.fold_in(arg_keys[4], 71), part),
    }


def subband_sum(slab, delays, length):

    def one_trial(row_delays):
        return jax.vmap(lambda channel_row, offset: lax.dynamic_slice_in_dim(channel_row, offset, length))(slab, row_delays)
    picked = jax.vmap(one_trial)(delays)
    return lax.optimization_barrier(jnp.sum(picked, axis=1, dtype=jnp.float32)).astype(jnp.bfloat16)

def dedisperse(series, delays, length):

    def one_trial(row_delays):
        return jax.vmap(lambda band_row, offset: lax.dynamic_slice_in_dim(band_row, offset, length))(series, row_delays)
    picked = jax.vmap(one_trial)(delays)
    return lax.optimization_barrier(jnp.sum(picked, axis=1, dtype=jnp.float32))

def peak_scores(normed, widths, span):
    running = jnp.concatenate([jnp.zeros((normed.shape[0], 1), normed.dtype), jnp.cumsum(normed, axis=1)], axis=1)

    def one_width(width):
        upper = lax.dynamic_slice_in_dim(running, width, span, 1)
        return lax.optimization_barrier(jnp.max((upper - running[:, :span]) / jnp.sqrt(width.astype(jnp.float32)), axis=1))
    return lax.map(one_width, widths).T

def reference(data, chan_delay, sub_delay, widths):
    tail_span = D1MAX + D2MAX + WMAX
    extended = jnp.concatenate([data, jnp.zeros((NCHAN, tail_span), jnp.bfloat16)], axis=1)
    sub_len = NT + D2MAX + WMAX
    channel_slabs = extended.reshape(NSUB, CPS, extended.shape[1])
    trial_delays = chan_delay.reshape(NSDM, NSUB, CPS).transpose(1, 0, 2)
    subband = lax.map(lambda members: subband_sum(members[0], members[1], sub_len), (channel_slabs, trial_delays))
    dm_len = NT + WMAX
    grouped = sub_delay.reshape(NSDM, DPS, NSUB)
    series = lax.map(lambda members: dedisperse(members[0], members[1], dm_len), (jnp.moveaxis(subband, 1, 0), grouped))
    series = series.reshape(NDM, dm_len)
    inside = series[:, :NT]
    average = lax.optimization_barrier(jnp.mean(inside, axis=1))
    deviation = jnp.sqrt(lax.optimization_barrier(jnp.mean((inside - average[:, None]) ** 2, axis=1)) + 1e-05)
    normed = (series - average[:, None]) / deviation[:, None]
    return peak_scores(normed, widths, NT)
```

```python
import functools

import jax
import jax.numpy as jnp
from jax import lax
from jax.experimental import pallas as pl
from jax.experimental.pallas import tpu as pltpu
from jax.sharding import PartitionSpec as P

NSUB = 64
NSDM = 64
WMAX = 256
CPS = 64
DPS = 32
D1MAX = 40
D2MAX = 24


def passed_along(value, axis, steps):
    count = lax.axis_size(axis)
    initial, last = (max(0, -steps), min(count, count - steps))
    return lax.ppermute(value, axis, [(source, source + steps) for source in range(initial, last)])


def shifted_sum(source, delays, length, largest):
    band_count = source.shape[0]
    trial_count = delays.shape[1]
    start_total = jnp.zeros((band_count, trial_count, length), jnp.float32)

    def add_shifts(step_index, running_total):
        for within in range(2):
            offset = 2 * step_index + within
            window = lax.dynamic_slice_in_dim(source, offset, length, 2)
            selector = (delays == offset).astype(jnp.bfloat16)
            running_total = running_total + jnp.einsum(
                "bsm,bmt->bst", selector, window, preferred_element_type=jnp.float32
            )
        return running_total

    return lax.fori_loop(0, (largest + 2) // 2, add_shifts, start_total)


def form_subbands(extended, chan_delay, length):
    band_count = extended.shape[0] // CPS
    channel_slabs = extended.reshape(band_count, CPS, extended.shape[1])
    trial_delays = chan_delay.reshape(NSDM, band_count, CPS).transpose(1, 0, 2)
    return shifted_sum(channel_slabs, trial_delays, length, D1MAX).astype(jnp.bfloat16)


def peak_scores(normed, widths, span):
    running = jnp.concatenate(
        [jnp.zeros((normed.shape[0], 1), normed.dtype), jnp.cumsum(normed, axis=1)], axis=1
    )

    def one_width(width):
        upper = lax.dynamic_slice_in_dim(running, width, span, 1)
        return jnp.max((upper - running[:, :span]) / jnp.sqrt(width.astype(jnp.float32)), axis=1)

    return lax.map(one_width, widths).T


def on_device(data, chan_delay, sub_delay, widths):
    block_len = data.shape[1]
    total_len = block_len * lax.axis_size("tm")
    edge_rows = passed_along(data[:, :D1MAX], "tm", -1)
    extended = jnp.concatenate([data, edge_rows], axis=1)
    subband = form_subbands(extended, chan_delay, block_len)
    regrouped = lax.all_to_all(subband, "freq", split_axis=1, concat_axis=0, tiled=True)
    later = passed_along(regrouped[:, :, : D2MAX + WMAX], "tm", -1)
    regrouped = jnp.concatenate([regrouped, later], axis=2)
    dm_len = block_len + WMAX
    local_trials = regrouped.shape[1]
    grouped = sub_delay.reshape(local_trials, DPS, NSUB)
    by_trial = jnp.transpose(regrouped, (1, 0, 2))
    series = shifted_sum(by_trial, grouped, dm_len, D2MAX)
    series = series.reshape(local_trials * DPS, dm_len)
    inside = series[:, :block_len]
    totals = lax.psum(jnp.sum(inside, axis=1), "tm")
    average = totals / total_len
    centred = lax.psum(jnp.sum((inside - average[:, None]) ** 2, axis=1), "tm")
    spread = centred / total_len
    deviation = jnp.sqrt(spread + 1e-05)
    normed = (series - average[:, None]) / deviation[:, None]
    local_peaks = peak_scores(normed, widths, block_len)
    return lax.pmax(local_peaks, "tm")


def fused_kernel(peers, block_len, data_ref, chan_ref, sub_ref, width_ref, out_ref,
                 times, shifted, select, product, outgoing, incoming,
                 running, send_sem, recv_sem, own_sem):
    me = lax.axis_index("freq")
    rows = data_ref.shape[0]
    bands = rows // CPS
    own_trials = NSDM // peers
    dms = sub_ref.shape[0]
    lanes = 2 * dms
    group = bands * own_trials
    f32, bf16 = jnp.float32, jnp.bfloat16

    barrier = pltpu.get_barrier_semaphore()

    def greet(step, carry):
        pl.semaphore_signal(barrier, inc=1, device_id={"freq": lax.rem(me + step, peers)},
                            device_id_type=pl.DeviceIdType.MESH)
        return carry

    lax.fori_loop(1, peers, greet, 0)

    def iota(shape, axis):
        return lax.broadcasted_iota(jnp.int32, shape, axis)

    def expand(delay_of, largest, width):
        for low in range(8):
            for high in range(largest // 8 + 1):
                if 8 * high + low > largest:
                    block = jnp.zeros((rows, width), bf16)
                else:
                    block = jnp.where(delay_of == float(8 * high + low), 1.0, 0.0).astype(bf16)
                select[low * rows:(low + 1) * rows, high * width:(high + 1) * width] = block

    def shifted_total(largest, width):
        highs = largest // 8 + 1
        length = block_len + 8 * highs
        for low in range(8):
            shifted[0:length, low * rows:(low + 1) * rows] = times[low:low + length, :].astype(bf16)
        for start in range(0, length, 128):
            stop = min(start + 128, length)
            product[start:stop, 0:highs * width] = jnp.dot(
                shifted[start:stop, :], select[:, 0:highs * width], preferred_element_type=f32)
        total = product[0:block_len, 0:width]
        for high in range(1, highs):
            total = total + product[8 * high:8 * high + block_len, high * width:(high + 1) * width]
        return total

    out_cols = NSDM * bands
    spread = (iota((NSDM, out_cols), 1) // bands == iota((NSDM, out_cols), 0)).astype(bf16)
    chan = chan_ref[...].astype(f32).astype(bf16)
    delay = lax.dot_general(chan, spread, (((0,), (0,)), ((), ())), preferred_element_type=f32)
    same = iota((rows, out_cols), 0) // CPS == iota((rows, out_cols), 1) % bands
    expand(jnp.where(same, delay, -1.0), D1MAX, out_cols)
    for start in range(0, block_len, 128):
        times[start:start + 128, :] = data_ref[:, start:start + 128].astype(f32).T
    times[block_len:, :] = jnp.zeros((times.shape[0] - block_len, rows), f32)
    subband = shifted_total(D1MAX, out_cols)
    for start in range(0, block_len, 128):
        block = subband[start:start + 128, :].T.astype(bf16)
        outgoing[:, :, start:start + 128] = block.reshape(peers, group, 128)

    pl.semaphore_wait(barrier, peers - 1)

    def sending(step):
        return pltpu.make_async_remote_copy(
            src_ref=outgoing.at[lax.rem(me + step, peers)], dst_ref=incoming.at[me],
            send_sem=send_sem.at[step], recv_sem=recv_sem.at[step],
            device_id={"freq": lax.rem(me + step, peers)}, device_id_type=pl.DeviceIdType.MESH)

    def start_one(step, carry):
        sending(step).start()
        return carry

    lax.fori_loop(1, peers, start_one, 0)
    own = pltpu.make_async_copy(outgoing.at[me], incoming.at[me], own_sem)
    own.start()

    trial_dms = dms // own_trials
    band_of = bands * (iota((rows, NSUB), 0) // group) + iota((rows, NSUB), 0) % bands
    pick = (band_of == iota((rows, NSUB), 1)).astype(bf16)
    sub = sub_ref[...].astype(f32).astype(bf16)
    sub = jnp.concatenate([sub, sub], axis=0)
    delay = lax.dot_general(pick, sub, (((1,), (1,)), ((), ())), preferred_element_type=f32)
    trial_of = (iota((rows, lanes), 0) % group) // bands
    same = trial_of == (iota((rows, lanes), 1) % dms) // trial_dms
    expand(jnp.where(same, delay, -1.0), D2MAX, lanes)
    below = iota((128, 256), 1) % 128 < iota((128, 256), 0)
    below = below.astype(f32).astype(bf16)

    def finish_one(step, carry):
        sending(step).wait()
        return carry

    own.wait()
    lax.fori_loop(1, peers, finish_one, 0)

    for start in range(0, block_len, 128):
        block = incoming[:, :, start:start + 128].reshape(rows, 128)
        times[start:start + 128, :] = block.astype(f32).T
    series = shifted_total(D2MAX, lanes)
    average = jnp.sum(series, axis=0, keepdims=True) / block_len
    centred = series - average
    spread = jnp.sum(centred * centred, axis=0, keepdims=True) / block_len
    deviation = jnp.sqrt(spread + 1e-05)
    carry = jnp.zeros((1, lanes), f32)
    for start in range(0, block_len, 128):
        block = centred[start:start + 128, :]
        head = block.astype(bf16)
        tail = (block - head.astype(f32)).astype(bf16)
        sums = jnp.dot(below, jnp.concatenate([head, tail], axis=0), preferred_element_type=f32) + carry
        running[start:start + 128, :] = sums
        carry = sums[127:128, :] + block[127:128, :]
    after = iota((WMAX, lanes), 0).astype(f32)
    running[block_len:block_len + WMAX, :] = carry - average * after

    half = block_len // 2
    left = iota((half + WMAX, lanes), 1) < dms
    running[0:half + WMAX, :] = jnp.where(left, running[0:half + WMAX, :], running[half:block_len + WMAX, :])
    base = running[0:half, :]
    peaks = []
    for index in range(width_ref.shape[0]):
        width = width_ref[index]
        upper = running[pl.ds(width, half), :]
        peak = jnp.max(upper - base, axis=0, keepdims=True)
        scale = jnp.sqrt(jnp.full((1, lanes), width.astype(f32)))
        peaks.append(peak / (deviation * scale))
    peaks = jnp.concatenate(peaks, axis=0)
    peaks = jnp.maximum(peaks, pltpu.roll(peaks, dms, 1))
    out_ref[...] = peaks[:, 0:dms]


def fused(data, chan_delay, sub_delay, widths):
    peers = lax.axis_size("freq")
    rows, block_len = data.shape
    bands = rows // CPS
    dms = sub_delay.shape[0]
    group = bands * (NSDM // peers)
    length = block_len + D1MAX + 8
    wide = (D1MAX // 8 + 1) * NSDM * bands
    vmem = pl.BlockSpec(memory_space=pltpu.VMEM)
    peaks = pl.pallas_call(
        functools.partial(fused_kernel, peers, block_len),
        out_shape=jax.ShapeDtypeStruct((widths.shape[0], dms), jnp.float32),
        in_specs=[vmem, vmem, vmem, pl.BlockSpec(memory_space=pltpu.SMEM)],
        out_specs=vmem,
        scratch_shapes=[
            pltpu.VMEM((length + 8, rows), jnp.float32),
            pltpu.VMEM((length, 8 * rows), jnp.bfloat16),
            pltpu.VMEM((8 * rows, wide), jnp.bfloat16),
            pltpu.VMEM((length, wide), jnp.float32),
            pltpu.VMEM((peers, group, block_len), jnp.bfloat16),
            pltpu.VMEM((peers, group, block_len), jnp.bfloat16),
            pltpu.VMEM((block_len + WMAX, 2 * dms), jnp.float32),
            pltpu.SemaphoreType.DMA((peers,)),
            pltpu.SemaphoreType.DMA((peers,)),
            pltpu.SemaphoreType.DMA,
        ],
        compiler_params=pltpu.CompilerParams(collective_id=0, has_side_effects=True),
    )(data, chan_delay, sub_delay, widths)
    return peaks.T


def solution(mesh):
    in_specs = (P(("beam", "freq"), "tm"), P(None, "freq"), P("freq", None), P())
    out_specs = P(("beam", "freq"), None)
    whole_time = mesh.shape["tm"] == 1
    return jax.shard_map(
        fused if whole_time else on_device, mesh=mesh, in_specs=in_specs, out_specs=out_specs, check_vma=False
    )
```

```python
import functools

import jax
import jax.numpy as jnp
from jax import lax
from jax.experimental import pallas as pl
from jax.experimental.pallas import tpu as pltpu
from jax.sharding import PartitionSpec as P

NSUB = 64
NSDM = 64
WMAX = 256
CPS = 64
DPS = 32
D1MAX = 40
D2MAX = 24


def passed_along(value, axis, steps):
    count = lax.axis_size(axis)
    initial, last = (max(0, -steps), min(count, count - steps))
    return lax.ppermute(value, axis, [(source, source + steps) for source in range(initial, last)])


def shifted_sum(source, delays, length, largest):
    band_count = source.shape[0]
    trial_count = delays.shape[1]
    start_total = jnp.zeros((band_count, trial_count, length), jnp.float32)

    def add_shifts(step_index, running_total):
        for within in range(2):
            offset = 2 * step_index + within
            window = lax.dynamic_slice_in_dim(source, offset, length, 2)
            selector = (delays == offset).astype(jnp.bfloat16)
            running_total = running_total + jnp.einsum(
                "bsm,bmt->bst", selector, window, preferred_element_type=jnp.float32
            )
        return running_total

    return lax.fori_loop(0, (largest + 2) // 2, add_shifts, start_total)


def form_subbands(extended, chan_delay, length):
    band_count = extended.shape[0] // CPS
    channel_slabs = extended.reshape(band_count, CPS, extended.shape[1])
    trial_delays = chan_delay.reshape(NSDM, band_count, CPS).transpose(1, 0, 2)
    return shifted_sum(channel_slabs, trial_delays, length, D1MAX).astype(jnp.bfloat16)


def peak_scores(normed, widths, span):
    running = jnp.concatenate(
        [jnp.zeros((normed.shape[0], 1), normed.dtype), jnp.cumsum(normed, axis=1)], axis=1
    )

    def one_width(width):
        upper = lax.dynamic_slice_in_dim(running, width, span, 1)
        return jnp.max((upper - running[:, :span]) / jnp.sqrt(width.astype(jnp.float32)), axis=1)

    return lax.map(one_width, widths).T


def on_device(data, chan_delay, sub_delay, widths):
    block_len = data.shape[1]
    total_len = block_len * lax.axis_size("tm")
    edge_rows = passed_along(data[:, :D1MAX], "tm", -1)
    extended = jnp.concatenate([data, edge_rows], axis=1)
    subband = form_subbands(extended, chan_delay, block_len)
    regrouped = lax.all_to_all(subband, "freq", split_axis=1, concat_axis=0, tiled=True)
    later = passed_along(regrouped[:, :, : D2MAX + WMAX], "tm", -1)
    regrouped = jnp.concatenate([regrouped, later], axis=2)
    dm_len = block_len + WMAX
    local_trials = regrouped.shape[1]
    grouped = sub_delay.reshape(local_trials, DPS, NSUB)
    by_trial = jnp.transpose(regrouped, (1, 0, 2))
    series = shifted_sum(by_trial, grouped, dm_len, D2MAX)
    series = series.reshape(local_trials * DPS, dm_len)
    inside = series[:, :block_len]
    totals = lax.psum(jnp.sum(inside, axis=1), "tm")
    average = totals / total_len
    centred = lax.psum(jnp.sum((inside - average[:, None]) ** 2, axis=1), "tm")
    spread = centred / total_len
    deviation = jnp.sqrt(spread + 1e-05)
    normed = (series - average[:, None]) / deviation[:, None]
    local_peaks = peak_scores(normed, widths, block_len)
    return lax.pmax(local_peaks, "tm")


def fused_kernel(peers, block_len, data_hbm, chan_hbm, sub_hbm, width_hbm, out_ref,
                 data_ref, chan_ref, sub_ref, width_ref, load_sem, times, shifted, select, product, outgoing, incoming,
                 running, send_sem, recv_sem, own_sem):
    me = lax.axis_index("freq")
    rows = data_ref.shape[0]
    bands = rows // CPS
    own_trials = NSDM // peers
    dms = sub_ref.shape[0]
    lanes = 2 * dms
    group = bands * own_trials
    f32, bf16 = jnp.float32, jnp.bfloat16

    barrier = pltpu.get_barrier_semaphore()

    def partner(step):
        if peers & (peers - 1):
            return lax.rem(me + step, peers)
        return lax.bitwise_xor(me, peers - step)

    def greet(step, carry):
        pl.semaphore_signal(barrier, inc=1, device_id={"freq": partner(step)},
                            device_id_type=pl.DeviceIdType.MESH)
        return carry

    lax.fori_loop(1, peers, greet, 0)
    loads = [
        pltpu.make_async_copy(source, target, load_sem.at[index])
        for index, (source, target) in enumerate((
            (chan_hbm, chan_ref), (data_hbm, data_ref), (sub_hbm, sub_ref), (width_hbm, width_ref)))
    ]
    for load in loads:
        load.start()

    def iota(shape, axis):
        return lax.broadcasted_iota(jnp.int32, shape, axis)

    def expand(delay_of, largest, width):
        for low in range(8):
            for high in range(largest // 8 + 1):
                if 8 * high + low > largest:
                    block = jnp.zeros((rows, width), bf16)
                else:
                    block = jnp.where(delay_of == float(8 * high + low), 1.0, 0.0).astype(bf16)
                select[low * rows:(low + 1) * rows, high * width:(high + 1) * width] = block

    def shifted_total(largest, width):
        highs = largest // 8 + 1
        length = block_len + 8 * highs
        for low in range(8):
            shifted[0:length, low * rows:(low + 1) * rows] = times[low:low + length, :].astype(bf16)
        for start in range(0, length, 128):
            stop = min(start + 128, length)
            product[start:stop, 0:highs * width] = jnp.dot(
                shifted[start:stop, :], select[:, 0:highs * width], preferred_element_type=f32)
        total = product[0:block_len, 0:width]
        for high in range(1, highs):
            total = total + product[8 * high:8 * high + block_len, high * width:(high + 1) * width]
        return total

    out_cols = NSDM * bands
    spread = (iota((NSDM, out_cols), 1) // bands == iota((NSDM, out_cols), 0)).astype(bf16)
    loads[0].wait()
    chan = chan_ref[...].astype(f32).astype(bf16)
    delay = lax.dot_general(chan, spread, (((0,), (0,)), ((), ())), preferred_element_type=f32)
    same = iota((rows, out_cols), 0) // CPS == iota((rows, out_cols), 1) % bands
    expand(jnp.where(same, delay, -1.0), D1MAX, out_cols)
    loads[1].wait()
    for start in range(0, block_len, 128):
        times[start:start + 128, :] = data_ref[:, start:start + 128].astype(f32).T
    times[block_len:, :] = jnp.zeros((times.shape[0] - block_len, rows), f32)
    subband = shifted_total(D1MAX, out_cols)
    for start in range(0, block_len, 128):
        block = subband[start:start + 128, :].T.astype(bf16)
        outgoing[:, :, start:start + 128] = block.reshape(peers, group, 128)

    pl.semaphore_wait(barrier, peers - 1)

    def sending(step):
        return pltpu.make_async_remote_copy(
            src_ref=outgoing.at[partner(step)], dst_ref=incoming.at[me],
            send_sem=send_sem.at[step], recv_sem=recv_sem.at[step],
            device_id={"freq": partner(step)}, device_id_type=pl.DeviceIdType.MESH)

    def start_one(step, carry):
        sending(step).start()
        return carry

    lax.fori_loop(1, peers, start_one, 0)
    own = pltpu.make_async_copy(outgoing.at[me], incoming.at[me], own_sem)
    own.start()

    trial_dms = dms // own_trials
    band_of = bands * (iota((rows, NSUB), 0) // group) + iota((rows, NSUB), 0) % bands
    pick = (band_of == iota((rows, NSUB), 1)).astype(bf16)
    loads[2].wait()
    loads[3].wait()
    sub = sub_ref[...].astype(f32).astype(bf16)
    sub = jnp.concatenate([sub, sub], axis=0)
    delay = lax.dot_general(pick, sub, (((1,), (1,)), ((), ())), preferred_element_type=f32)
    trial_of = (iota((rows, lanes), 0) % group) // bands
    same = trial_of == (iota((rows, lanes), 1) % dms) // trial_dms
    expand(jnp.where(same, delay, -1.0), D2MAX, lanes)
    below = iota((128, 256), 1) % 128 < iota((128, 256), 0)
    below = below.astype(f32).astype(bf16)

    def finish_one(step, carry):
        sending(step).wait()
        return carry

    own.wait()
    lax.fori_loop(1, peers, finish_one, 0)

    for start in range(0, block_len, 128):
        block = incoming[:, :, start:start + 128].reshape(rows, 128)
        times[start:start + 128, :] = block.astype(f32).T
    series = shifted_total(D2MAX, lanes)
    average = jnp.sum(series, axis=0, keepdims=True) / block_len
    centred = series - average
    spread = jnp.sum(centred * centred, axis=0, keepdims=True) / block_len
    deviation = jnp.sqrt(spread + 1e-05)
    carry = jnp.zeros((1, lanes), f32)
    for start in range(0, block_len, 128):
        block = centred[start:start + 128, :]
        head = block.astype(bf16)
        tail = (block - head.astype(f32)).astype(bf16)
        sums = jnp.dot(below, jnp.concatenate([head, tail], axis=0), preferred_element_type=f32) + carry
        running[start:start + 128, :] = sums
        carry = sums[127:128, :] + block[127:128, :]
    after = iota((WMAX, lanes), 0).astype(f32)
    running[block_len:block_len + WMAX, :] = carry - average * after

    half = block_len // 2
    left = iota((half + WMAX, lanes), 1) < dms
    running[0:half + WMAX, :] = jnp.where(left, running[0:half + WMAX, :], running[half:block_len + WMAX, :])
    base = running[0:half, :]
    peaks = []
    for index in range(width_ref.shape[0]):
        width = width_ref[index]
        upper = running[pl.ds(width, half), :]
        peak = jnp.max(upper - base, axis=0, keepdims=True)
        scale = jnp.sqrt(jnp.full((1, lanes), width.astype(f32)))
        peaks.append(peak / (deviation * scale))
    peaks = jnp.concatenate(peaks, axis=0)
    peaks = jnp.maximum(peaks, pltpu.roll(peaks, dms, 1))
    out_ref[...] = peaks[:, 0:dms]


def fused(data, chan_delay, sub_delay, widths):
    peers = lax.axis_size("freq")
    rows, block_len = data.shape
    bands = rows // CPS
    dms = sub_delay.shape[0]
    group = bands * (NSDM // peers)
    length = block_len + D1MAX + 8
    wide = (D1MAX // 8 + 1) * NSDM * bands
    anywhere = pl.BlockSpec(memory_space=pl.ANY)
    peaks = pl.pallas_call(
        functools.partial(fused_kernel, peers, block_len),
        out_shape=pltpu.VMEM((widths.shape[0], dms), jnp.float32),
        in_specs=[anywhere] * 4,
        out_specs=pl.BlockSpec(memory_space=pltpu.VMEM),
        scratch_shapes=[
            pltpu.VMEM(data.shape, data.dtype),
            pltpu.VMEM(chan_delay.shape, chan_delay.dtype),
            pltpu.VMEM(sub_delay.shape, sub_delay.dtype),
            pltpu.SMEM(widths.shape, widths.dtype),
            pltpu.SemaphoreType.DMA((4,)),
            pltpu.VMEM((length + 8, rows), jnp.float32),
            pltpu.VMEM((length, 8 * rows), jnp.bfloat16),
            pltpu.VMEM((8 * rows, wide), jnp.bfloat16),
            pltpu.VMEM((length, wide), jnp.float32),
            pltpu.VMEM((peers, group, block_len), jnp.bfloat16),
            pltpu.VMEM((peers, group, block_len), jnp.bfloat16),
            pltpu.VMEM((block_len + WMAX, 2 * dms), jnp.float32),
            pltpu.SemaphoreType.DMA((peers,)),
            pltpu.SemaphoreType.DMA((peers,)),
            pltpu.SemaphoreType.DMA,
        ],
        compiler_params=pltpu.CompilerParams(collective_id=0, has_side_effects=True),
    )(data, chan_delay, sub_delay, widths)
    return peaks.T


def solution(mesh):
    in_specs = (P(("beam", "freq"), "tm"), P(None, "freq"), P("freq", None), P())
    out_specs = P(("beam", "freq"), None)
    whole_time = mesh.shape["tm"] == 1
    return jax.shard_map(
        fused if whole_time else on_device, mesh=mesh, in_specs=in_specs, out_specs=out_specs, check_vma=False
    )
```

```python
import functools

import jax
import jax.numpy as jnp
from jax import lax
from jax.experimental import pallas as pl
from jax.experimental.pallas import tpu as pltpu
from jax.sharding import PartitionSpec as P

NSUB = 64
NSDM = 64
WMAX = 256
CPS = 64
DPS = 32
D1MAX = 40
D2MAX = 24


def passed_along(value, axis, steps):
    count = lax.axis_size(axis)
    initial, last = (max(0, -steps), min(count, count - steps))
    return lax.ppermute(value, axis, [(source, source + steps) for source in range(initial, last)])


def shifted_sum(source, delays, length, largest):
    band_count = source.shape[0]
    trial_count = delays.shape[1]
    start_total = jnp.zeros((band_count, trial_count, length), jnp.float32)

    def add_shifts(step_index, running_total):
        for within in range(2):
            offset = 2 * step_index + within
            window = lax.dynamic_slice_in_dim(source, offset, length, 2)
            selector = (delays == offset).astype(jnp.bfloat16)
            running_total = running_total + jnp.einsum(
                "bsm,bmt->bst", selector, window, preferred_element_type=jnp.float32
            )
        return running_total

    return lax.fori_loop(0, (largest + 2) // 2, add_shifts, start_total)


def form_subbands(extended, chan_delay, length):
    band_count = extended.shape[0] // CPS
    channel_slabs = extended.reshape(band_count, CPS, extended.shape[1])
    trial_delays = chan_delay.reshape(NSDM, band_count, CPS).transpose(1, 0, 2)
    return shifted_sum(channel_slabs, trial_delays, length, D1MAX).astype(jnp.bfloat16)


def peak_scores(normed, widths, span):
    running = jnp.concatenate(
        [jnp.zeros((normed.shape[0], 1), normed.dtype), jnp.cumsum(normed, axis=1)], axis=1
    )

    def one_width(width):
        upper = lax.dynamic_slice_in_dim(running, width, span, 1)
        return jnp.max((upper - running[:, :span]) / jnp.sqrt(width.astype(jnp.float32)), axis=1)

    return lax.map(one_width, widths).T


def on_device(data, chan_delay, sub_delay, widths):
    block_len = data.shape[1]
    total_len = block_len * lax.axis_size("tm")
    edge_rows = passed_along(data[:, :D1MAX], "tm", -1)
    extended = jnp.concatenate([data, edge_rows], axis=1)
    subband = form_subbands(extended, chan_delay, block_len)
    regrouped = lax.all_to_all(subband, "freq", split_axis=1, concat_axis=0, tiled=True)
    later = passed_along(regrouped[:, :, : D2MAX + WMAX], "tm", -1)
    regrouped = jnp.concatenate([regrouped, later], axis=2)
    dm_len = block_len + WMAX
    local_trials = regrouped.shape[1]
    grouped = sub_delay.reshape(local_trials, DPS, NSUB)
    by_trial = jnp.transpose(regrouped, (1, 0, 2))
    series = shifted_sum(by_trial, grouped, dm_len, D2MAX)
    series = series.reshape(local_trials * DPS, dm_len)
    inside = series[:, :block_len]
    totals = lax.psum(jnp.sum(inside, axis=1), "tm")
    average = totals / total_len
    centred = lax.psum(jnp.sum((inside - average[:, None]) ** 2, axis=1), "tm")
    spread = centred / total_len
    deviation = jnp.sqrt(spread + 1e-05)
    normed = (series - average[:, None]) / deviation[:, None]
    local_peaks = peak_scores(normed, widths, block_len)
    return lax.pmax(local_peaks, "tm")


def fused_kernel(peers, block_len, data_hbm, chan_hbm, sub_hbm, width_hbm, out_ref,
                 data_ref, chan_ref, sub_ref, width_ref, load_sem, times, shifted, select, product, outgoing, incoming,
                 running, send_sem, recv_sem, own_sem):
    me = lax.axis_index("freq")
    rows = data_ref.shape[0]
    bands = rows // CPS
    own_trials = NSDM // peers
    dms = sub_ref.shape[0]
    lanes = 2 * dms
    group = bands * own_trials
    f32, bf16 = jnp.float32, jnp.bfloat16

    barrier = pltpu.get_barrier_semaphore()

    def partner(step):
        return lax.rem(me + step, peers)

    def greet(step, carry):
        pl.semaphore_signal(barrier, inc=1, device_id={"freq": partner(step)},
                            device_id_type=pl.DeviceIdType.MESH)
        return carry

    lax.fori_loop(1, peers, greet, 0)
    loads = [
        pltpu.make_async_copy(source, target, load_sem.at[index])
        for index, (source, target) in enumerate((
            (chan_hbm, chan_ref), (data_hbm, data_ref), (sub_hbm, sub_ref), (width_hbm, width_ref)))
    ]
    for load in loads:
        load.start()

    def iota(shape, axis):
        return lax.broadcasted_iota(jnp.int32, shape, axis)

    def expand(delay_of, largest, width):
        for low in range(8):
            for high in range(largest // 8 + 1):
                if 8 * high + low > largest:
                    block = jnp.zeros((rows, width), bf16)
                else:
                    block = jnp.where(delay_of == float(8 * high + low), 1.0, 0.0).astype(bf16)
                select[low * rows:(low + 1) * rows, high * width:(high + 1) * width] = block

    def products(largest, width):
        highs = largest // 8 + 1
        length = block_len + 8 * highs
        for low in range(8):
            shifted[0:length, low * rows:(low + 1) * rows] = times[low:low + length, :].astype(bf16)
        for start in range(0, length, 128):
            stop = min(start + 128, length)
            product[start:stop, 0:highs * width] = jnp.dot(
                shifted[start:stop, :], select[:, 0:highs * width], preferred_element_type=f32)

    def shifted_total(largest, width):
        highs = largest // 8 + 1
        products(largest, width)
        total = product[0:block_len, 0:width]
        for high in range(1, highs):
            total = total + product[8 * high:8 * high + block_len, high * width:(high + 1) * width]
        return total

    out_cols = NSDM * bands
    spread = (iota((NSDM, out_cols), 1) // bands == iota((NSDM, out_cols), 0)).astype(bf16)
    loads[0].wait()
    chan = chan_ref[...].astype(f32).astype(bf16)
    delay = lax.dot_general(chan, spread, (((0,), (0,)), ((), ())), preferred_element_type=f32)
    same = iota((rows, out_cols), 0) // CPS == iota((rows, out_cols), 1) % bands
    expand(jnp.where(same, delay, -1.0), D1MAX, out_cols)
    loads[1].wait()
    for start in range(0, block_len, 128):
        times[start:start + 128, :] = data_ref[:, start:start + 128].astype(f32).T
    times[block_len:, :] = jnp.zeros((times.shape[0] - block_len, rows), f32)
    subband = shifted_total(D1MAX, out_cols)
    for start in range(0, block_len, 128):
        block = subband[start:start + 128, :].T.astype(bf16)
        outgoing[:, :, start:start + 128] = block.reshape(peers, group, 128)

    pl.semaphore_wait(barrier, peers - 1)

    def sending(step):
        return pltpu.make_async_remote_copy(
            src_ref=outgoing.at[partner(step)], dst_ref=incoming.at[me],
            send_sem=send_sem.at[step], recv_sem=recv_sem.at[step],
            device_id={"freq": partner(step)}, device_id_type=pl.DeviceIdType.MESH)

    def start_one(step, carry):
        sending(step).start()
        return carry

    lax.fori_loop(1, peers, start_one, 0)
    own = pltpu.make_async_copy(outgoing.at[me], incoming.at[me], own_sem)
    own.start()

    trial_dms = dms // own_trials
    band_of = bands * (iota((rows, NSUB), 0) // group) + iota((rows, NSUB), 0) % bands
    pick = (band_of == iota((rows, NSUB), 1)).astype(bf16)
    loads[2].wait()
    loads[3].wait()
    sub = sub_ref[...].astype(f32).astype(bf16)
    delay = lax.dot_general(pick, sub, (((1,), (1,)), ((), ())), preferred_element_type=f32)
    trial_of = (iota((rows, dms), 0) % group) // bands
    same = trial_of == iota((rows, dms), 1) // trial_dms
    expand(jnp.where(same, delay, -1.0), D2MAX, dms)
    below = iota((128, 256), 1) % 128 < iota((128, 256), 0)
    below = below.astype(f32).astype(bf16)

    def finish_one(step, carry):
        sending(step).wait()
        return carry

    own.wait()
    lax.fori_loop(1, peers, finish_one, 0)

    for start in range(0, block_len, 128):
        block = incoming[:, :, start:start + 128].reshape(rows, 128)
        times[start:start + 128, :] = block.astype(f32).T
    products(D2MAX, dms)
    pairs = (D2MAX // 8 + 1) // 2
    mixed = product[0:block_len + 8, 0:lanes]
    for pair in range(1, pairs):
        mixed = mixed + product[16 * pair:16 * pair + block_len + 8, pair * lanes:(pair + 1) * lanes]
    swapped = pltpu.roll(mixed, dms, 1)
    on_left = iota((block_len, lanes), 1) < dms
    series = (jnp.where(on_left, mixed[0:block_len], swapped[0:block_len])
              + jnp.where(on_left, swapped[8:], mixed[8:]))
    average = jnp.sum(series, axis=0, keepdims=True) / block_len
    centred = series - average
    spread = jnp.sum(centred * centred, axis=0, keepdims=True) / block_len
    deviation = jnp.sqrt(spread + 1e-05)
    carry = jnp.zeros((1, lanes), f32)
    for start in range(0, block_len, 128):
        block = centred[start:start + 128, :]
        head = block.astype(bf16)
        tail = (block - head.astype(f32)).astype(bf16)
        sums = jnp.dot(below, jnp.concatenate([head, tail], axis=0), preferred_element_type=f32) + carry
        running[start:start + 128, :] = sums
        carry = sums[127:128, :] + block[127:128, :]
    after = iota((WMAX, lanes), 0).astype(f32)
    running[block_len:block_len + WMAX, :] = carry - average * after

    half = block_len // 2
    left = iota((half + WMAX, lanes), 1) < dms
    running[0:half + WMAX, :] = jnp.where(left, running[0:half + WMAX, :], running[half:block_len + WMAX, :])
    base = running[0:half, :]
    peaks = []
    for index in range(width_ref.shape[0]):
        width = width_ref[index]
        upper = running[pl.ds(width, half), :]
        peak = jnp.max(upper - base, axis=0, keepdims=True)
        scale = jnp.sqrt(jnp.full((1, lanes), width.astype(f32)))
        peaks.append(peak / (deviation * scale))
    peaks = jnp.concatenate(peaks, axis=0)
    peaks = jnp.maximum(peaks, pltpu.roll(peaks, dms, 1))
    out_ref[...] = peaks[:, 0:dms]


def fused(data, chan_delay, sub_delay, widths):
    peers = lax.axis_size("freq")
    rows, block_len = data.shape
    bands = rows // CPS
    dms = sub_delay.shape[0]
    group = bands * (NSDM // peers)
    length = block_len + D1MAX + 8
    wide = (D1MAX // 8 + 1) * NSDM * bands
    anywhere = pl.BlockSpec(memory_space=pl.ANY)
    peaks = pl.pallas_call(
        functools.partial(fused_kernel, peers, block_len),
        out_shape=pltpu.VMEM((widths.shape[0], dms), jnp.float32),
        in_specs=[anywhere] * 4,
        out_specs=pl.BlockSpec(memory_space=pltpu.VMEM),
        scratch_shapes=[
            pltpu.VMEM(data.shape, data.dtype),
            pltpu.VMEM(chan_delay.shape, chan_delay.dtype),
            pltpu.VMEM(sub_delay.shape, sub_delay.dtype),
            pltpu.SMEM(widths.shape, widths.dtype),
            pltpu.SemaphoreType.DMA((4,)),
            pltpu.VMEM((length + 8, rows), jnp.float32),
            pltpu.VMEM((length, 8 * rows), jnp.bfloat16),
            pltpu.VMEM((8 * rows, wide), jnp.bfloat16),
            pltpu.VMEM((length, wide), jnp.float32),
            pltpu.VMEM((peers, group, block_len), jnp.bfloat16),
            pltpu.VMEM((peers, group, block_len), jnp.bfloat16),
            pltpu.VMEM((block_len + WMAX, 2 * dms), jnp.float32),
            pltpu.SemaphoreType.DMA((peers,)),
            pltpu.SemaphoreType.DMA((peers,)),
            pltpu.SemaphoreType.DMA,
        ],
        compiler_params=pltpu.CompilerParams(collective_id=0, has_side_effects=True),
    )(data, chan_delay, sub_delay, widths)
    return peaks.T


def solution(mesh):
    in_specs = (P(("beam", "freq"), "tm"), P(None, "freq"), P("freq", None), P())
    out_specs = P(("beam", "freq"), None)
    whole_time = mesh.shape["tm"] == 1
    return jax.shard_map(
        fused if whole_time else on_device, mesh=mesh, in_specs=in_specs, out_specs=out_specs, check_vma=False
    )
```

```python
import functools

import jax
import jax.numpy as jnp
from jax import lax
from jax.experimental import pallas as pl
from jax.experimental.pallas import tpu as pltpu
from jax.sharding import PartitionSpec as P

NSUB = 64
NSDM = 64
WMAX = 256
CPS = 64
DPS = 32
D1MAX = 40
D2MAX = 24


def passed_along(value, axis, steps):
    count = lax.axis_size(axis)
    initial, last = (max(0, -steps), min(count, count - steps))
    return lax.ppermute(value, axis, [(source, source + steps) for source in range(initial, last)])


def shifted_sum(source, delays, length, largest):
    band_count = source.shape[0]
    trial_count = delays.shape[1]
    start_total = jnp.zeros((band_count, trial_count, length), jnp.float32)

    def add_shifts(step_index, running_total):
        for within in range(2):
            offset = 2 * step_index + within
            window = lax.dynamic_slice_in_dim(source, offset, length, 2)
            selector = (delays == offset).astype(jnp.bfloat16)
            running_total = running_total + jnp.einsum(
                "bsm,bmt->bst", selector, window, preferred_element_type=jnp.float32
            )
        return running_total

    return lax.fori_loop(0, (largest + 2) // 2, add_shifts, start_total)


def form_subbands(extended, chan_delay, length):
    band_count = extended.shape[0] // CPS
    channel_slabs = extended.reshape(band_count, CPS, extended.shape[1])
    trial_delays = chan_delay.reshape(NSDM, band_count, CPS).transpose(1, 0, 2)
    return shifted_sum(channel_slabs, trial_delays, length, D1MAX).astype(jnp.bfloat16)


def peak_scores(normed, widths, span):
    running = jnp.concatenate(
        [jnp.zeros((normed.shape[0], 1), normed.dtype), jnp.cumsum(normed, axis=1)], axis=1
    )

    def one_width(width):
        upper = lax.dynamic_slice_in_dim(running, width, span, 1)
        return jnp.max((upper - running[:, :span]) / jnp.sqrt(width.astype(jnp.float32)), axis=1)

    return lax.map(one_width, widths).T


def on_device(data, chan_delay, sub_delay, widths):
    block_len = data.shape[1]
    total_len = block_len * lax.axis_size("tm")
    edge_rows = passed_along(data[:, :D1MAX], "tm", -1)
    extended = jnp.concatenate([data, edge_rows], axis=1)
    subband = form_subbands(extended, chan_delay, block_len)
    regrouped = lax.all_to_all(subband, "freq", split_axis=1, concat_axis=0, tiled=True)
    later = passed_along(regrouped[:, :, : D2MAX + WMAX], "tm", -1)
    regrouped = jnp.concatenate([regrouped, later], axis=2)
    dm_len = block_len + WMAX
    local_trials = regrouped.shape[1]
    grouped = sub_delay.reshape(local_trials, DPS, NSUB)
    by_trial = jnp.transpose(regrouped, (1, 0, 2))
    series = shifted_sum(by_trial, grouped, dm_len, D2MAX)
    series = series.reshape(local_trials * DPS, dm_len)
    inside = series[:, :block_len]
    totals = lax.psum(jnp.sum(inside, axis=1), "tm")
    average = totals / total_len
    centred = lax.psum(jnp.sum((inside - average[:, None]) ** 2, axis=1), "tm")
    spread = centred / total_len
    deviation = jnp.sqrt(spread + 1e-05)
    normed = (series - average[:, None]) / deviation[:, None]
    local_peaks = peak_scores(normed, widths, block_len)
    return lax.pmax(local_peaks, "tm")


def fused_kernel(peers, block_len, data_hbm, chan_hbm, sub_hbm, width_hbm, out_ref,
                 data_ref, chan_ref, sub_ref, width_ref, load_sem, times, shifted, select, product, outgoing, incoming,
                 running, send_sem, recv_sem, own_sem):
    me = lax.axis_index("freq")
    rows = data_ref.shape[0]
    bands = rows // CPS
    own_trials = NSDM // peers
    dms = sub_ref.shape[0]
    lanes = 2 * dms
    group = bands * own_trials
    f32, bf16 = jnp.float32, jnp.bfloat16

    barrier = pltpu.get_barrier_semaphore()

    def partner(step):
        return lax.rem(me + step, peers)

    def greet(step, carry):
        pl.semaphore_signal(barrier, inc=1, device_id={"freq": partner(step)},
                            device_id_type=pl.DeviceIdType.MESH)
        return carry

    lax.fori_loop(1, peers, greet, 0)
    loads = [
        pltpu.make_async_copy(source, target, load_sem.at[index])
        for index, (source, target) in enumerate((
            (chan_hbm, chan_ref), (data_hbm, data_ref), (sub_hbm, sub_ref), (width_hbm, width_ref)))
    ]
    for load in loads:
        load.start()

    def iota(shape, axis):
        return lax.broadcasted_iota(jnp.int32, shape, axis)

    def expand(delay_of, largest, width):
        for low in range(8):
            for high in range(largest // 8 + 1):
                if 8 * high + low > largest:
                    block = jnp.zeros((rows, width), bf16)
                else:
                    block = jnp.where(delay_of == float(8 * high + low), 1.0, 0.0).astype(bf16)
                select[low * rows:(low + 1) * rows, high * width:(high + 1) * width] = block

    def products(largest, width):
        highs = largest // 8 + 1
        length = block_len + 8 * highs
        for low in range(8):
            shifted[0:length, low * rows:(low + 1) * rows] = times[low:low + length, :].astype(bf16)
        for start in range(0, length, 352):
            stop = min(start + 352, length)
            product[start:stop, 0:highs * width] = jnp.dot(
                shifted[start:stop, :], select[:, 0:highs * width], preferred_element_type=f32)

    def shifted_total(largest, width):
        highs = largest // 8 + 1
        products(largest, width)
        total = product[0:block_len, 0:width]
        for high in range(1, highs):
            total = total + product[8 * high:8 * high + block_len, high * width:(high + 1) * width]
        return total

    out_cols = NSDM * bands
    spread = (iota((NSDM, out_cols), 1) // bands == iota((NSDM, out_cols), 0)).astype(bf16)
    loads[0].wait()
    chan = chan_ref[...].astype(f32).astype(bf16)
    delay = lax.dot_general(chan, spread, (((0,), (0,)), ((), ())), preferred_element_type=f32)
    same = iota((rows, out_cols), 0) // CPS == iota((rows, out_cols), 1) % bands
    expand(jnp.where(same, delay, -1.0), D1MAX, out_cols)
    loads[1].wait()
    for start in range(0, block_len, 128):
        times[start:start + 128, :] = data_ref[:, start:start + 128].astype(f32).T
    times[block_len:, :] = jnp.zeros((times.shape[0] - block_len, rows), f32)
    subband = shifted_total(D1MAX, out_cols)
    for start in range(0, block_len, 128):
        block = subband[start:start + 128, :].T.astype(bf16)
        outgoing[:, :, start:start + 128] = block.reshape(peers, group, 128)

    pl.semaphore_wait(barrier, peers - 1)

    def sending(step):
        return pltpu.make_async_remote_copy(
            src_ref=outgoing.at[partner(step)], dst_ref=incoming.at[me],
            send_sem=send_sem.at[step], recv_sem=recv_sem.at[step],
            device_id={"freq": partner(step)}, device_id_type=pl.DeviceIdType.MESH)

    def start_one(step, carry):
        sending(step).start()
        return carry

    lax.fori_loop(1, peers, start_one, 0)
    own = pltpu.make_async_copy(outgoing.at[me], incoming.at[me], own_sem)
    own.start()

    trial_dms = dms // own_trials
    band_of = bands * (iota((rows, NSUB), 0) // group) + iota((rows, NSUB), 0) % bands
    pick = (band_of == iota((rows, NSUB), 1)).astype(bf16)
    loads[2].wait()
    loads[3].wait()
    sub = sub_ref[...].astype(f32).astype(bf16)
    delay = lax.dot_general(pick, sub, (((1,), (1,)), ((), ())), preferred_element_type=f32)
    trial_of = (iota((rows, dms), 0) % group) // bands
    same = trial_of == iota((rows, dms), 1) // trial_dms
    expand(jnp.where(same, delay, -1.0), D2MAX, dms)
    below = iota((128, 256), 1) % 128 < iota((128, 256), 0)
    below = below.astype(f32).astype(bf16)

    def finish_one(step, carry):
        sending(step).wait()
        return carry

    own.wait()
    lax.fori_loop(1, peers, finish_one, 0)

    for start in range(0, block_len, 128):
        block = incoming[:, :, start:start + 128].reshape(rows, 128)
        times[start:start + 128, :] = block.astype(f32).T
    products(D2MAX, dms)
    pairs = (D2MAX // 8 + 1) // 2
    mixed = product[0:block_len + 8, 0:lanes]
    for pair in range(1, pairs):
        mixed = mixed + product[16 * pair:16 * pair + block_len + 8, pair * lanes:(pair + 1) * lanes]
    swapped = pltpu.roll(mixed, dms, 1)
    on_left = iota((block_len, lanes), 1) < dms
    series = (jnp.where(on_left, mixed[0:block_len], swapped[0:block_len])
              + jnp.where(on_left, swapped[8:], mixed[8:]))
    average = jnp.sum(series, axis=0, keepdims=True) / block_len
    centred = series - average
    spread = jnp.sum(centred * centred, axis=0, keepdims=True) / block_len
    deviation = jnp.sqrt(spread + 1e-05)
    carry = jnp.zeros((1, lanes), f32)
    for start in range(0, block_len, 128):
        block = centred[start:start + 128, :]
        head = block.astype(bf16)
        tail = (block - head.astype(f32)).astype(bf16)
        sums = jnp.dot(below, jnp.concatenate([head, tail], axis=0), preferred_element_type=f32) + carry
        running[start:start + 128, :] = sums
        carry = sums[127:128, :] + block[127:128, :]
    after = iota((WMAX, lanes), 0).astype(f32)
    running[block_len:block_len + WMAX, :] = carry - average * after

    half = block_len // 2
    left = iota((half + WMAX, lanes), 1) < dms
    running[0:half + WMAX, :] = jnp.where(left, running[0:half + WMAX, :], running[half:block_len + WMAX, :])
    base = running[0:half, :]
    peaks = []
    for index in range(width_ref.shape[0]):
        width = width_ref[index]
        upper = running[pl.ds(width, half), :]
        peak = jnp.max(upper - base, axis=0, keepdims=True)
        scale = jnp.sqrt(jnp.full((1, lanes), width.astype(f32)))
        peaks.append(peak / (deviation * scale))
    peaks = jnp.concatenate(peaks, axis=0)
    peaks = jnp.maximum(peaks, pltpu.roll(peaks, dms, 1))
    out_ref[...] = peaks[:, 0:dms]


def fused(data, chan_delay, sub_delay, widths):
    peers = lax.axis_size("freq")
    rows, block_len = data.shape
    bands = rows // CPS
    dms = sub_delay.shape[0]
    group = bands * (NSDM // peers)
    length = block_len + D1MAX + 8
    wide = (D1MAX // 8 + 1) * NSDM * bands
    anywhere = pl.BlockSpec(memory_space=pl.ANY)
    peaks = pl.pallas_call(
        functools.partial(fused_kernel, peers, block_len),
        out_shape=pltpu.VMEM((widths.shape[0], dms), jnp.float32),
        in_specs=[anywhere] * 4,
        out_specs=pl.BlockSpec(memory_space=pltpu.VMEM),
        scratch_shapes=[
            pltpu.VMEM(data.shape, data.dtype),
            pltpu.VMEM(chan_delay.shape, chan_delay.dtype),
            pltpu.VMEM(sub_delay.shape, sub_delay.dtype),
            pltpu.SMEM(widths.shape, widths.dtype),
            pltpu.SemaphoreType.DMA((4,)),
            pltpu.VMEM((length + 8, rows), jnp.float32),
            pltpu.VMEM((length, 8 * rows), jnp.bfloat16),
            pltpu.VMEM((8 * rows, wide), jnp.bfloat16),
            pltpu.VMEM((length, wide), jnp.float32),
            pltpu.VMEM((peers, group, block_len), jnp.bfloat16),
            pltpu.VMEM((peers, group, block_len), jnp.bfloat16),
            pltpu.VMEM((block_len + WMAX, 2 * dms), jnp.float32),
            pltpu.SemaphoreType.DMA((peers,)),
            pltpu.SemaphoreType.DMA((peers,)),
            pltpu.SemaphoreType.DMA,
        ],
        compiler_params=pltpu.CompilerParams(collective_id=0, has_side_effects=True),
    )(data, chan_delay, sub_delay, widths)
    return peaks.T


def solution(mesh):
    in_specs = (P(("beam", "freq"), "tm"), P(None, "freq"), P("freq", None), P())
    out_specs = P(("beam", "freq"), None)
    whole_time = mesh.shape["tm"] == 1
    return jax.shard_map(
        fused if whole_time else on_device, mesh=mesh, in_specs=in_specs, out_specs=out_specs, check_vma=False
    )
```
